512 devices in a mesh: dp: 32 (over z_lo, x), mp: 16 (over z_hi, y, core).
Axes of the slice: x: 4, y: 4, z: 16 (z_hi: 2, z_lo: 8; z = z_hi * 8 + z_lo), core: 2. Of those that a mesh axis runs over, the one named last changes fastest.
Arguments:
- x_tiles: bfloat16 [32768, 6144], P('dp', 'mp')
- counts: int32 [32, 32], replicated, may hold values from 4 to 28, as said below
- owners: int32 [32, 32], replicated, may hold values from 0 to 31, as said below
- ln_gain: bfloat16 [6144], P('mp'), may hold values from 0.5 to 1.5
- w_up: bfloat16 [6144, 12288], P('dp', 'mp'), may hold values from -0.078125 to 0.078125
- up_bias: bfloat16 [12288], P('mp'), may hold values from -3 to 3
Outputs:
- hidden_act: bfloat16 [16384, 12288], P('dp', 'mp')
The draws below stay inside these ranges and needn't reach their ends.
Inputs may be any that keep to these rules, and one draw needn't show every extreme that they name: Each row of owners is a permutation of 0 .. 31. Tile t of group s holds counts[s, t] patches in its first slots; every group takes exactly 512 patches in all.
All inputs are finite; a program needn't handle non-finite values.
Results may differ from the reference program's by a relative error of at most 0.0047.
Values may be sent and summed in bfloat16 or wider, within the bound.
No kernel may reach another device: no remote copies, remote signals or barrier semaphores. Data moves between devices by JAX's collectives and lax.ppermute only.
A program may use at most 64 MiB of HBM per device.

```python
import jax
import jax.numpy as jnp
from jax import lax

D = 6144
HID = 12288
RECV = 512
GROUPS = 32
TILE_ROWS = 32


def level_offsets(ranks, amplitude, groups):
    upper = amplitude * (2 * ranks - (groups - 1)) // (groups - 1)
    lower = -(amplitude * (2 * (groups - 1 - ranks) - (groups - 1)) // (groups - 1))
    return jnp.where(2 * ranks >= groups, upper, lower)


def routing(key):
    groups = GROUPS
    share = RECV // groups
    base_key = jax.random.fold_in(key, 7)
    key_rank, key_noise, key_owner = jax.random.split(base_key, 3)
    source_rank = jax.random.permutation(key_rank, groups).astype(jnp.int32)
    noise_keys = jax.random.split(key_noise, groups)
    noise_rank = jax.vmap(lambda single: jax.random.permutation(single, groups))(noise_keys).astype(jnp.int32)
    first_row = jnp.arange(groups, dtype=jnp.int32)[:, None] == 0
    noise_rank = jnp.where(first_row, source_rank[None, :], noise_rank)
    matrix = share + level_offsets(source_rank, share // 2, groups)[:, None] + level_offsets(noise_rank, share // 4, groups).T
    owner_keys = jax.random.split(key_owner, groups)
    owners = jax.vmap(lambda single: jax.random.permutation(single, groups))(owner_keys).astype(jnp.int32)
    counts = jnp.take_along_axis(matrix, owners, axis=1).astype(jnp.int32)
    return (owners, counts)


def draw_owners(key, part):
    return routing(key)[0]


def draw_counts(key, part):
    return routing(key)[1]


def draw_x_tiles(key, part):
    total_rows = GROUPS * GROUPS * TILE_ROWS
    key_col, key_row, key_off, key_val = jax.random.split(jax.random.fold_in(key, 11), 4)
    position = jnp.arange(D, dtype=jnp.float32) / D
    col_scale = jnp.power(10.0, position) * (0.6 + 0.8 * jax.random.uniform(key_col, (1, D), jnp.float32))
    row_scale = jnp.power(10.0, jax.random.uniform(key_row, (total_rows, 1), jnp.float32))
    offset = jax.random.normal(key_off, (total_rows, 1), jnp.float32)
    values = jax.random.normal(key_val, (total_rows, D), jnp.float32)
    result = (values + offset) * row_scale * col_scale
    return result.astype(jnp.bfloat16)


def steps_of(rng, shape, cuts, low, high):
    level, own = 1.0, jax.random.fold_in(rng, 6)
    for axis_at, parts in cuts:
        draws = jnp.exp(jax.random.uniform(jax.random.fold_in(own, axis_at), (parts,), jnp.float32, low / len(cuts), high / len(cuts)))
        level = level * jnp.repeat(draws, shape[axis_at] // parts).reshape([-1 if axis == axis_at else 1 for axis in range(len(shape))])
    return level


def scatter_about(own_key, extent, spread, bound, cuts=(), kind=jnp.bfloat16):
    values = spread * jax.random.normal(own_key, extent, jnp.float32)
    if cuts:
        values = values * steps_of(own_key, extent, cuts, -0.22, 0.18)
    return jnp.clip(values, -bound, bound).astype(kind)


def setup_inputs(seed: int = 0) -> dict:
    key_of = jax.random.split(jax.random.key(seed), 7)
    x_tiles = draw_x_tiles(jax.random.fold_in(key_of[6], 71), 0)
    counts = draw_counts(jax.random.fold_in(key_of[6], 71), 0)
    owners = draw_owners(jax.random.fold_in(key_of[6], 71), 0)
    ln_gain = jnp.clip(1.0 + 0.1 * jax.random.normal(key_of[3], (D,), jnp.float32), 0.5, 1.5).astype(jnp.bfloat16)
    w_up = scatter_about(key_of[4], (D, HID), D ** -0.5, 0.078125, ((0, 32), (1, 16)))
    up_bias = scatter_about(key_of[5], (HID,), 0.5, 3.0, ((0, 16),))
    return {"x_tiles": x_tiles, "counts": counts, "owners": owners, "ln_gain": ln_gain, "w_up": w_up, "up_bias": up_bias}


def pack_index(counts, owners, target):
    inverse = jnp.argsort(owners, axis=1).astype(jnp.int32)
    tile_index = lax.dynamic_index_in_dim(inverse, target, 1, keepdims=False).astype(jnp.int32)
    counted = jnp.take_along_axis(counts, tile_index[:, None], axis=1)[:, 0]
    inclusive = jnp.cumsum(counted).astype(jnp.int32)
    exclusive = inclusive - counted
    positions = jnp.arange(RECV, dtype=jnp.int32)
    source = lax.optimization_barrier(jnp.sum((inclusive[None, :] <= positions[:, None]).astype(jnp.int32), axis=1)).astype(jnp.int32)
    slot_index = positions - jnp.take(exclusive, source)
    return ((source * GROUPS + jnp.take(tile_index, source)) * TILE_ROWS + slot_index).astype(jnp.int32)

def layer_norm(packed_rows, ln_gain):
    as_float = packed_rows.astype(jnp.float32)
    row_mean = lax.optimization_barrier(jnp.mean(as_float, axis=1, keepdims=True))
    row_square = lax.optimization_barrier(jnp.mean(as_float * as_float, axis=1, keepdims=True))
    variance = row_square - row_mean * row_mean
    scaled = (as_float - row_mean) * lax.rsqrt(variance + 1e-06) * ln_gain.astype(jnp.float32)
    return scaled.astype(jnp.bfloat16)

def reference(x_tiles, counts, owners, ln_gain, w_up, up_bias):

    def per_group(target):
        row_index = pack_index(counts, owners, target)
        packed_rows = jnp.take(x_tiles, row_index, axis=0)
        normed = layer_norm(packed_rows, ln_gain)
        preact = jnp.dot(normed, w_up, preferred_element_type=jnp.float32) + up_bias.astype(jnp.float32)
        return jax.nn.gelu(preact, approximate=False).astype(jnp.bfloat16)
    blocks = lax.map(per_group, jnp.arange(GROUPS, dtype=jnp.int32))
    return blocks.reshape(GROUPS * RECV, HID)
```

```python
import functools

import jax
import jax.numpy as jnp
from jax import lax
from jax.experimental import pallas as pl
from jax.experimental.pallas import tpu as pltpu
from jax.sharding import Mesh, PartitionSpec as P

D = 6144
RECV = 512
PART = 384
BLOCK = 192
HALF = BLOCK // 2
COLS = 768
GAIN_ROWS = 16
ROWS = RECV + GAIN_ROWS
STRIP = 32
INV_SQRT2 = 0.7071067811865476


def shift(value, axis, size, step):
    return lax.ppermute(value, axis, [(i, (i + step) % size) for i in range(size)])


def row_copies(x, pieces, w_all, sems):
    copies = []
    for half in range(2):
        own, below, above, far_a, far_b = pieces[5 * half : 5 * half + 5]
        sources = [(own, z, 0, z) for z in range(8)]
        sources += [(below, z, 3, z) for z in range(8)]
        sources += [(above, z, 1, z) for z in range(8)]
        sources += [(far_a, z, 2, z) for z in range(4)]
        sources += [(far_b, z - 4, 2, z) for z in range(4, 8)]
        for ref, at, step, z in sources:
            block = 4 * z + lax.rem(x + step, 4)
            start = pl.multiple_of(block * BLOCK + half * HALF, 32)
            copies.append(
                pltpu.make_async_copy(
                    ref.at[pl.ds(at * HALF, HALF), :],
                    w_all.at[pl.ds(start, HALF), :],
                    sems.at[len(copies)],
                )
            )
    return copies


def mlp_kernel(place_ref, near_ref, far_ref, bias_ref, *refs):
    pieces, (out_ref, w_all, normed, sems) = refs[:10], refs[10:]
    x, half = place_ref[0], place_ref[1]
    copies = row_copies(x, pieces, w_all, sems)
    for copy in copies:
        copy.start()

    chunks = [
        (ref, c, y, side)
        for side, ref in enumerate((near_ref, far_ref))
        for y in range(4)
        for c in range(2)
    ]

    @pl.loop(0, RECV // STRIP)
    def _(strip):
        rows = pl.ds(pl.multiple_of(strip * STRIP, STRIP), STRIP)
        total = jnp.zeros((STRIP, 128), jnp.float32)
        square = jnp.zeros((STRIP, 128), jnp.float32)
        for ref, c, y, _side in chunks:
            for lane in range(PART // 128):
                v = ref[c, y, rows, lane * 128 : (lane + 1) * 128].astype(jnp.float32)
                total += v
                square += v * v
        row_mean = jnp.sum(total, axis=1, keepdims=True) / D
        variance = jnp.sum(square, axis=1, keepdims=True) / D - row_mean * row_mean
        scale = lax.rsqrt(variance + 1e-06)
        for ref, c, y, side in chunks:
            v = ref[c, y, rows, :].astype(jnp.float32)
            gain = ref[c, y, RECV : RECV + 1, :].astype(jnp.float32)
            at = 8 * lax.rem(half + side, 2) + 2 * y + c
            columns = pl.ds(pl.multiple_of(at * PART, 128), PART)
            normed[rows, columns] = ((v - row_mean) * scale * gain).astype(jnp.bfloat16)

    for copy in copies:
        copy.wait()
    for n in range(COLS // 256):
        cols = slice(n * 256, (n + 1) * 256)
        v = jnp.dot(normed[...], w_all[:, cols], preferred_element_type=jnp.float32)
        v = v + bias_ref[:, cols].astype(jnp.float32)
        out_ref[:, cols] = (v * (1.0 + lax.erf(v * INV_SQRT2)) * 0.5).astype(jnp.bfloat16)


def mlp(place, near, far, bias, pieces):
    vmem = pl.BlockSpec(memory_space=pltpu.VMEM)
    return pl.pallas_call(
        mlp_kernel,
        out_shape=jax.ShapeDtypeStruct((RECV, COLS), jnp.bfloat16),
        in_specs=[pl.BlockSpec(memory_space=pltpu.SMEM), vmem, vmem, vmem]
        + [pl.BlockSpec(memory_space=pl.ANY)] * len(pieces),
        out_specs=vmem,
        scratch_shapes=[
            pltpu.VMEM((D, COLS), jnp.bfloat16),
            pltpu.VMEM((RECV, D), jnp.bfloat16),
            pltpu.SemaphoreType.DMA((64,)),
        ],
        compiler_params=pltpu.CompilerParams(vmem_limit_bytes=44 * 1024 * 1024),
        cost_estimate=pl.CostEstimate(
            flops=2 * RECV * D * COLS, bytes_accessed=2 * (RECV * D + D * COLS), transcendentals=RECV * COLS
        ),
    )(place, near, far, bias, *pieces)


def gather_weight(w_half):
    own = lax.all_gather(w_half, "zl", axis=0, tiled=True)
    below = shift(own, "x", 4, 1)
    above = shift(own, "x", 4, -1)
    middle = own.shape[0] // 2
    return [own, below, above, shift(below[:middle], "x", 4, 1), shift(above[middle:], "x", 4, -1)]


def spread(rows):
    copies = jnp.broadcast_to(rows[None], (4,) + rows.shape)
    along_y = lax.all_to_all(copies, "y", split_axis=0, concat_axis=0, tiled=True)
    return lax.all_gather(along_y, "c", axis=0)


def local(x_tiles, counts, owners, ln_gain, w_up, up_bias):
    pieces = gather_weight(w_up[:HALF]) + gather_weight(w_up[HALF:])

    groups = 32
    my_index = lax.axis_index("zl") * 4 + lax.axis_index("x")
    slots = x_tiles.shape[0] // groups
    tile_block = x_tiles.reshape(groups, slots, PART)
    inverse = jnp.argsort(owners, axis=1)
    my_tiles = lax.dynamic_index_in_dim(inverse, my_index, 0, keepdims=False)
    outgoing = jnp.take(tile_block, my_tiles, axis=0)
    incoming = lax.all_to_all(outgoing, ("zl", "x"), split_axis=0, concat_axis=0, tiled=True)
    source_tiles = lax.dynamic_index_in_dim(inverse, my_index, 1, keepdims=False)
    held_rows = jnp.take_along_axis(counts, source_tiles[:, None], axis=1)[:, 0]
    inclusive = jnp.cumsum(held_rows)
    exclusive = inclusive - held_rows
    positions = jnp.arange(RECV, dtype=jnp.int32)
    source = jnp.sum((inclusive[None, :] <= positions[:, None]).astype(jnp.int32), axis=1)
    slot_index = positions - jnp.take(exclusive, source)
    flat_index = source * slots + slot_index
    packed = jnp.take(incoming.reshape(groups * slots, PART), flat_index, axis=0)

    gains = jnp.broadcast_to(ln_gain[None, :], (GAIN_ROWS, PART))
    mine = jnp.concatenate([packed, gains], axis=0)
    other = shift(mine, "zh", 2, 1)
    near, far = spread(mine), spread(other)
    place = jnp.stack([lax.axis_index("x"), lax.axis_index("zh")]).astype(jnp.int32)
    return mlp(place, near, far, up_bias[None, :], pieces)


def solution(mesh):
    fine = Mesh(mesh.devices.reshape(8, 4, 2, 4, 2), ("zl", "x", "zh", "y", "c"))
    dp, mp = ("zl", "x"), ("zh", "y", "c")
    return jax.shard_map(
        local,
        mesh=fine,
        in_specs=(P(dp, mp), P(), P(), P(mp), P(dp, mp), P(mp)),
        out_specs=P(dp, mp),
        check_vma=False,
    )
```

```python
import functools

import jax
import jax.numpy as jnp
from jax import lax
from jax.experimental import pallas as pl
from jax.experimental.pallas import tpu as pltpu
from jax.sharding import Mesh, PartitionSpec as P

D = 6144
RECV = 512
PART = 384
BLOCK = 192
COLS = 768
GAIN_ROWS = 16
ROWS = RECV + GAIN_ROWS
STRIP = 32
INV_SQRT2 = 0.7071067811865476


def shift(value, axis, size, step):
    return lax.ppermute(value, axis, [(i, (i + step) % size) for i in range(size)])


def row_copies(place_ref, pieces, w_all, sems):
    own, below, above, far_a, far_b = pieces
    x = place_ref[0]
    copies = []
    for z in range(8):
        far = far_a if z < 4 else far_b
        for ref, at, step in ((own, z, 0), (below, z, 3), (above, z, 1), (far, z % 4, 2)):
            block = 4 * z + lax.rem(x + step, 4)
            copies.append(
                pltpu.make_async_copy(
                    ref.at[pl.ds(at * BLOCK, BLOCK), :],
                    w_all.at[pl.ds(pl.multiple_of(block * BLOCK, 64), BLOCK), :],
                    sems.at[len(copies)],
                )
            )
    return copies


def mlp_kernel(place_ref, *refs):
    rows_refs, bias_ref, pieces = refs[:2], refs[2], refs[3:8]
    out_ref, w_all, normed, sems = refs[8:]
    half = place_ref[1]
    copies = row_copies(place_ref, pieces, w_all, sems)
    for copy in copies:
        copy.start()

    chunks = [
        (rows_refs[side], part, 8 * lax.rem(half + side, 2) + part)
        for side in range(2)
        for part in range(8)
    ]

    @pl.loop(0, RECV // STRIP)
    def _(strip):
        rows = pl.ds(pl.multiple_of(strip * STRIP, STRIP), STRIP)
        total = jnp.zeros((STRIP, 128), jnp.float32)
        square = jnp.zeros((STRIP, 128), jnp.float32)
        for ref, part, _at in chunks:
            for lane in range(PART // 128):
                v = ref[part, rows, lane * 128 : (lane + 1) * 128].astype(jnp.float32)
                total += v
                square += v * v
        row_mean = jnp.sum(total, axis=1, keepdims=True) / D
        variance = jnp.sum(square, axis=1, keepdims=True) / D - row_mean * row_mean
        scale = lax.rsqrt(variance + 1e-06)
        for ref, part, at in chunks:
            v = ref[part, rows, :].astype(jnp.float32)
            gain = ref[part, RECV : RECV + 1, :].astype(jnp.float32)
            columns = pl.ds(pl.multiple_of(at * PART, 128), PART)
            normed[rows, columns] = ((v - row_mean) * scale * gain).astype(jnp.bfloat16)

    for copy in copies:
        copy.wait()
    for n in range(COLS // 256):
        cols = slice(n * 256, (n + 1) * 256)
        v = jnp.dot(normed[...], w_all[:, cols], preferred_element_type=jnp.float32)
        v = v + bias_ref[:, cols].astype(jnp.float32)
        out_ref[:, cols] = (v * (1.0 + lax.erf(v * INV_SQRT2)) * 0.5).astype(jnp.bfloat16)


def mlp(place, rows, bias, pieces):
    vmem = pl.BlockSpec(memory_space=pltpu.VMEM)
    return pl.pallas_call(
        mlp_kernel,
        out_shape=jax.ShapeDtypeStruct((RECV, COLS), jnp.bfloat16),
        in_specs=[pl.BlockSpec(memory_space=pltpu.SMEM)]
        + [vmem] * 3
        + [pl.BlockSpec(memory_space=pl.ANY)] * len(pieces),
        out_specs=vmem,
        scratch_shapes=[
            pltpu.VMEM((D, COLS), jnp.bfloat16),
            pltpu.VMEM((RECV, D), jnp.bfloat16),
            pltpu.SemaphoreType.DMA((32,)),
        ],
        compiler_params=pltpu.CompilerParams(vmem_limit_bytes=26 * 1024 * 1024),
        cost_estimate=pl.CostEstimate(
            flops=2 * RECV * D * COLS, bytes_accessed=2 * (RECV * D + D * COLS), transcendentals=RECV * COLS
        ),
    )(place, *rows, bias, *pieces)


def beside(own):
    return [shift(own, "x", 4, 1), shift(own, "x", 4, -1)]


def across(below, above):
    middle = below.shape[0] // 2
    return [shift(below[:middle], "x", 4, 1), shift(above[middle:], "x", 4, -1)]


def together(*lists):
    return lax.optimization_barrier(tuple(lists))


def local(x_tiles, counts, owners, ln_gain, w_up, up_bias):
    own = lax.all_gather(w_up, "zl", axis=0, tiled=True)
    near = beside(own)
    far = across(*near)

    groups = 32
    my_index = lax.axis_index(("zl", "x"))
    slots = x_tiles.shape[0] // groups
    tile_block = x_tiles.reshape(groups, slots, PART)
    inverse = jnp.argsort(owners, axis=1)
    my_tiles = lax.dynamic_index_in_dim(inverse, my_index, 0, keepdims=False)
    outgoing = jnp.take(tile_block, my_tiles, axis=0)
    source_tiles = lax.dynamic_index_in_dim(inverse, my_index, 1, keepdims=False)
    held_rows = jnp.take_along_axis(counts, source_tiles[:, None], axis=1)[:, 0]
    inclusive = jnp.cumsum(held_rows)
    exclusive = inclusive - held_rows
    positions = jnp.arange(RECV, dtype=jnp.int32)
    source = jnp.sum((inclusive[None, :] <= positions[:, None]).astype(jnp.int32), axis=1)
    slot_index = positions - jnp.take(exclusive, source)
    flat_index = source * slots + slot_index
    outgoing, flat_index = together(outgoing, flat_index)
    incoming = lax.all_to_all(outgoing, ("zl", "x"), split_axis=0, concat_axis=0, tiled=True)
    packed = jnp.take(incoming.reshape(groups * slots, PART), flat_index, axis=0)

    gains = jnp.broadcast_to(ln_gain[None, :], (GAIN_ROWS, PART))
    mine = jnp.concatenate([packed, gains], axis=0)
    other = shift(mine, "zh", 2, 1)
    other, near = together(other, near)
    pieces = [own, *near, *far]
    rows = [lax.all_gather(part, ("y", "c"), axis=0) for part in (mine, other)]
    axes = [lax.axis_index(axis) for axis in ("x", "zh")]
    return mlp(jnp.stack(axes).astype(jnp.int32), rows, up_bias[None, :], pieces)


def solution(mesh):
    fine = Mesh(mesh.devices.reshape(8, 4, 2, 4, 2), ("zl", "x", "zh", "y", "c"))
    dp, mp = ("zl", "x"), ("zh", "y", "c")
    return jax.shard_map(
        local,
        mesh=fine,
        in_specs=(P(dp, mp), P(), P(), P(mp), P(dp, mp), P(mp)),
        out_specs=P(dp, mp),
        check_vma=False,
    )
```

```python
import functools

import jax
import jax.numpy as jnp
from jax import lax
from jax.experimental import pallas as pl
from jax.experimental.pallas import tpu as pltpu
from jax.sharding import Mesh, PartitionSpec as P

D = 6144
RECV = 512
PART = 384
BLOCK = 192
COLS = 768
GAIN_ROWS = 16
ROWS = RECV + GAIN_ROWS
STRIP = 32
VMEM_MIB = 60
INV_SQRT2 = 0.7071067811865476


def shift(value, axis, size, step):
    return lax.ppermute(value, axis, [(i, (i + step) % size) for i in range(size)])


def row_copies(place_ref, pieces, w_ref, sems):
    here, own, below, above, far_a, far_b = pieces
    x, z_lo = place_ref[0], place_ref[2]

    def block(at, count):
        return pl.ds(pl.multiple_of(at * BLOCK, 64), count * BLOCK)

    copies = [pltpu.make_async_copy(here, w_ref.at[block(4 * z_lo, 4), :], sems.at[28])]
    for slot in range(7):
        at = jnp.where(z_lo == slot, 7, slot)
        far = far_a if slot < 4 else far_b
        for ref, row, step in ((own, slot, 0), (below, slot, 3), (above, slot, 1), (far, slot % 4, 2)):
            copies.append(
                pltpu.make_async_copy(
                    ref.at[pl.ds(row * BLOCK, BLOCK), :],
                    w_ref.at[block(4 * at + lax.rem(x + step, 4), 1), :],
                    sems.at[len(copies) - 1],
                )
            )
    return copies


def mlp_kernel(place_ref, near_ref, far_ref, bias_ref, *refs):
    pieces, (out_ref, rows_ref, w_ref, normed_ref, row_sems, sems) = refs[:6], refs[6:]
    half = place_ref[1]
    inward = [
        pltpu.make_async_copy(ref, rows_ref.at[pl.ds(8 * side, 8)], row_sems.at[side])
        for side, ref in enumerate((near_ref, far_ref))
    ]
    copies = row_copies(place_ref, pieces, w_ref, sems)
    for copy in inward + copies:
        copy.start()
    for copy in inward:
        copy.wait()

    @pl.loop(0, RECV // STRIP)
    def _(strip):
        rows = pl.ds(pl.multiple_of(strip * STRIP, STRIP), STRIP)
        total = jnp.zeros((STRIP, 128), jnp.float32)
        square = jnp.zeros((STRIP, 128), jnp.float32)
        for index in range(16):
            for lane in range(PART // 128):
                v = rows_ref[index, rows, lane * 128 : (lane + 1) * 128].astype(jnp.float32)
                total += v
                square += v * v
        row_mean = jnp.sum(total, axis=1, keepdims=True) / D
        variance = jnp.sum(square, axis=1, keepdims=True) / D - row_mean * row_mean
        scale = lax.rsqrt(variance + 1e-06)
        for index in range(16):
            v = rows_ref[index, rows, :].astype(jnp.float32)
            gain = rows_ref[index, RECV : RECV + 1, :].astype(jnp.float32)
            at = 8 * lax.rem(half + index // 8, 2) + index % 8
            columns = pl.ds(pl.multiple_of(at * PART, 128), PART)
            normed_ref[rows, columns] = ((v - row_mean) * scale * gain).astype(jnp.bfloat16)

    for copy in copies:
        copy.wait()
    for n in range(COLS // 256):
        cols = slice(n * 256, (n + 1) * 256)
        v = jnp.dot(normed_ref[...], w_ref[:, cols], preferred_element_type=jnp.float32)
        v = v + bias_ref[:, cols].astype(jnp.float32)
        out_ref[:, cols] = (v * (1.0 + lax.erf(v * INV_SQRT2)) * 0.5).astype(jnp.bfloat16)


def mlp(place, rows, bias, pieces):
    vmem = pl.BlockSpec(memory_space=pltpu.VMEM)
    left = pl.BlockSpec(memory_space=pl.ANY)
    return pl.pallas_call(
        mlp_kernel,
        out_shape=jax.ShapeDtypeStruct((RECV, COLS), jnp.bfloat16),
        in_specs=[pl.BlockSpec(memory_space=pltpu.SMEM)] + [left] * 2 + [vmem] + [left] * 6,
        out_specs=vmem,
        scratch_shapes=[
            pltpu.VMEM((16, ROWS, PART), jnp.bfloat16),
            pltpu.VMEM((D, COLS), jnp.bfloat16),
            pltpu.VMEM((RECV, D), jnp.bfloat16),
            pltpu.SemaphoreType.DMA((2,)),
            pltpu.SemaphoreType.DMA((29,)),
        ],
        compiler_params=pltpu.CompilerParams(vmem_limit_bytes=VMEM_MIB * 1024 * 1024),
        cost_estimate=pl.CostEstimate(
            flops=2 * RECV * D * COLS, bytes_accessed=2 * (RECV * D + D * COLS), transcendentals=RECV * COLS
        ),
    )(place, *rows, bias, *pieces)


def beside(own):
    return [shift(own, "x", 4, 1), shift(own, "x", 4, -1)]


def across(below, above):
    middle = 4 * BLOCK
    return [shift(below[:middle], "x", 4, 1), shift(above[middle:], "x", 4, -1)]


def together(*lists):
    return lax.optimization_barrier(tuple(lists))


def local(x_tiles, counts, owners, ln_gain, w_up, up_bias):
    z_lo = lax.axis_index("zl")
    copies = jnp.broadcast_to(w_up[None], (4, BLOCK, COLS))
    here = lax.all_to_all(copies, "x", split_axis=0, concat_axis=0, tiled=True).reshape(4 * BLOCK, COLS)
    own = lax.all_gather(w_up, "zl", axis=0, tiled=True)
    own = lax.dynamic_update_slice(own, own[7 * BLOCK :], (z_lo * BLOCK, 0))[: 7 * BLOCK]
    near = beside(own)
    far = across(*near)

    groups = 32
    my_index = lax.axis_index(("zl", "x"))
    slots = x_tiles.shape[0] // groups
    tile_block = x_tiles.reshape(groups, slots, PART)
    inverse = jnp.argsort(owners, axis=1)
    my_tiles = lax.dynamic_index_in_dim(inverse, my_index, 0, keepdims=False)
    outgoing = jnp.take(tile_block, my_tiles, axis=0)
    source_tiles = lax.dynamic_index_in_dim(inverse, my_index, 1, keepdims=False)
    held_rows = jnp.take_along_axis(counts, source_tiles[:, None], axis=1)[:, 0]
    inclusive = jnp.cumsum(held_rows)
    exclusive = inclusive - held_rows
    positions = jnp.arange(RECV, dtype=jnp.int32)
    source = jnp.sum((inclusive[None, :] <= positions[:, None]).astype(jnp.int32), axis=1)
    chosen = source[:, None] == jnp.arange(groups, dtype=jnp.int32)[None, :]
    slot_index = positions - jnp.sum(jnp.where(chosen, exclusive[None, :], 0), axis=1)
    flat_index = source * slots + slot_index
    outgoing, flat_index, here = together(outgoing, flat_index, here)
    incoming = lax.all_to_all(outgoing, ("zl", "x"), split_axis=0, concat_axis=0, tiled=True)
    packed = jnp.take(incoming.reshape(groups * slots, PART), flat_index, axis=0)

    gains = jnp.broadcast_to(ln_gain[None, :], (GAIN_ROWS, PART))
    mine = jnp.concatenate([packed, gains], axis=0)
    other = shift(mine, "zh", 2, 1)
    other, near = together(other, near)
    pieces = [here, own, *near, *far]
    rows = [lax.all_gather(part, ("y", "c"), axis=0) for part in (mine, other)]
    axes = [lax.axis_index(axis) for axis in ("x", "zh", "zl")]
    return mlp(jnp.stack(axes).astype(jnp.int32), rows, up_bias[None, :], pieces)


def solution(mesh):
    fine = Mesh(mesh.devices.reshape(8, 4, 2, 4, 2), ("zl", "x", "zh", "y", "c"))
    dp, mp = ("zl", "x"), ("zh", "y", "c")
    return jax.shard_map(
        local,
        mesh=fine,
        in_specs=(P(dp, mp), P(), P(), P(mp), P(dp, mp), P(mp)),
        out_specs=P(dp, mp),
        check_vma=False,
    )
```

```python
import functools

import jax
import jax.numpy as jnp
from jax import lax
from jax.experimental import pallas as pl
from jax.experimental.pallas import tpu as pltpu
from jax.sharding import Mesh, PartitionSpec as P

D = 6144
RECV = 512
PART = 384
BLOCK = 192
COLS = 768
GAIN_ROWS = 16
ROWS = RECV + GAIN_ROWS
STRIP = 32
CHUNK = 128
NEAR_MIB = 58
VMEM_MIB = 60
INV_SQRT2 = 0.7071067811865476


def shift(value, axis, size, step):
    return lax.ppermute(value, axis, [(i, (i + step) % size) for i in range(size)])


def row_copies(place_ref, pieces, w_ref, sems):
    here, own, below, above, far_a, far_b = pieces
    x, z_lo = place_ref[0], place_ref[2]

    def block(at, count):
        return pl.ds(pl.multiple_of(at * BLOCK, 64), count * BLOCK)

    copies = [pltpu.make_async_copy(here, w_ref.at[block(4 * z_lo, 4), :], sems.at[28])]
    for slot in range(7):
        at = jnp.where(z_lo == slot, 7, slot)
        far = far_a if slot < 4 else far_b
        for ref, row, step in ((own, slot, 0), (below, slot, 3), (above, slot, 1), (far, slot % 4, 2)):
            copies.append(
                pltpu.make_async_copy(
                    ref.at[pl.ds(row * BLOCK, BLOCK), :],
                    w_ref.at[block(4 * at + lax.rem(x + step, 4), 1), :],
                    sems.at[len(copies) - 1],
                )
            )
    return copies


def row_sums(rows_ref, first, rows, total, square):
    for index in range(first, first + 8):
        for lane in range(PART // 128):
            v = rows_ref[index, rows, lane * 128 : (lane + 1) * 128].astype(jnp.float32)
            total += v
            square += v * v
    return total, square


def near_kernel(near_ref, sums_ref, rows_ref, sem):
    inward = pltpu.make_async_copy(near_ref, rows_ref, sem)
    inward.start()
    inward.wait()

    @pl.loop(0, RECV // STRIP)
    def _(strip):
        rows = pl.ds(pl.multiple_of(strip * STRIP, STRIP), STRIP)
        zero = jnp.zeros((STRIP, 128), jnp.float32)
        sums_ref[0, rows, :], sums_ref[1, rows, :] = row_sums(rows_ref, 0, rows, zero, zero)


def mlp_kernel(place_ref, sums_ref, near_ref, far_ref, bias_ref, *refs):
    pieces, (out_ref, rows_ref, w_ref, normed_ref, row_sems, sems) = refs[:6], refs[6:]
    half = place_ref[1]
    blocks = [pl.ds(RECV, GAIN_ROWS)] + [pl.ds(i * CHUNK, CHUNK) for i in range(RECV // CHUNK)]
    inward = [
        pltpu.make_async_copy(ref.at[:, block, :], rows_ref.at[pl.ds(8 * side, 8), block, :], row_sems.at[2 * i + side])
        for i, block in enumerate(blocks)
        for side, ref in enumerate((near_ref, far_ref))
    ]
    copies = row_copies(place_ref, pieces, w_ref, sems)
    for copy in inward + copies:
        copy.start()
    inward[0].wait()
    inward[1].wait()
    for chunk in range(RECV // CHUNK):
        inward[2 + 2 * chunk].wait()
        inward[3 + 2 * chunk].wait()

        @pl.loop(chunk * (CHUNK // STRIP), (chunk + 1) * (CHUNK // STRIP))
        def _(strip):
            rows = pl.ds(pl.multiple_of(strip * STRIP, STRIP), STRIP)
            total, square = row_sums(rows_ref, 8, rows, sums_ref[0, rows, :], sums_ref[1, rows, :])
            row_mean = jnp.sum(total, axis=1, keepdims=True) / D
            variance = jnp.sum(square, axis=1, keepdims=True) / D - row_mean * row_mean
            scale = lax.rsqrt(variance + 1e-06)
            for index in range(16):
                v = rows_ref[index, rows, :].astype(jnp.float32)
                gain = rows_ref[index, RECV : RECV + 1, :].astype(jnp.float32)
                at = 8 * lax.rem(half + index // 8, 2) + index % 8
                columns = pl.ds(pl.multiple_of(at * PART, 128), PART)
                normed_ref[rows, columns] = ((v - row_mean) * scale * gain).astype(jnp.bfloat16)

    for copy in copies:
        copy.wait()
    for n in range(COLS // 256):
        cols = slice(n * 256, (n + 1) * 256)
        v = jnp.dot(normed_ref[...], w_ref[:, cols], preferred_element_type=jnp.float32)
        v = v + bias_ref[:, cols].astype(jnp.float32)
        out_ref[:, cols] = (v * (1.0 + lax.erf(v * INV_SQRT2)) * 0.5).astype(jnp.bfloat16)


def mlp(place, rows, bias, pieces):
    near, far = rows
    vmem = pl.BlockSpec(memory_space=pltpu.VMEM)
    left = pl.BlockSpec(memory_space=pl.ANY)
    sums = pl.pallas_call(
        near_kernel,
        out_shape=jax.ShapeDtypeStruct((2, RECV, 128), jnp.float32),
        in_specs=[left],
        out_specs=vmem,
        scratch_shapes=[pltpu.VMEM((8, ROWS, PART), jnp.bfloat16), pltpu.SemaphoreType.DMA],
        compiler_params=pltpu.CompilerParams(vmem_limit_bytes=NEAR_MIB * 1024 * 1024),
        cost_estimate=pl.CostEstimate(flops=2 * RECV * D, bytes_accessed=2 * RECV * D, transcendentals=0),
    )(near)
    return pl.pallas_call(
        mlp_kernel,
        out_shape=jax.ShapeDtypeStruct((RECV, COLS), jnp.bfloat16),
        in_specs=[pl.BlockSpec(memory_space=pltpu.SMEM), vmem, left, left, vmem] + [left] * 6,
        out_specs=vmem,
        scratch_shapes=[
            pltpu.VMEM((16, ROWS, PART), jnp.bfloat16),
            pltpu.VMEM((D, COLS), jnp.bfloat16),
            pltpu.VMEM((RECV, D), jnp.bfloat16),
            pltpu.SemaphoreType.DMA((10,)),
            pltpu.SemaphoreType.DMA((29,)),
        ],
        compiler_params=pltpu.CompilerParams(vmem_limit_bytes=VMEM_MIB * 1024 * 1024),
        cost_estimate=pl.CostEstimate(
            flops=2 * RECV * D * COLS, bytes_accessed=2 * (RECV * D + D * COLS), transcendentals=RECV * COLS
        ),
    )(place, sums, near, far, bias, *pieces)


def beside(own):
    return [shift(own, "x", 4, 1), shift(own, "x", 4, -1)]


def across(below, above):
    middle = 4 * BLOCK
    return [shift(below[:middle], "x", 4, 1), shift(above[middle:], "x", 4, -1)]


def together(*lists):
    return lax.optimization_barrier(tuple(lists))


def local(x_tiles, counts, owners, ln_gain, w_up, up_bias):
    z_lo = lax.axis_index("zl")
    copies = jnp.broadcast_to(w_up[None], (4, BLOCK, COLS))
    here = lax.all_to_all(copies, "x", split_axis=0, concat_axis=0, tiled=True).reshape(4 * BLOCK, COLS)
    own = lax.all_gather(w_up, "zl", axis=0, tiled=True)
    own = lax.dynamic_update_slice(own, own[7 * BLOCK :], (z_lo * BLOCK, 0))[: 7 * BLOCK]
    near = beside(own)
    far = across(*near)

    groups = 32
    my_index = lax.axis_index(("zl", "x"))
    slots = x_tiles.shape[0] // groups
    tile_block = x_tiles.reshape(groups, slots, PART)
    inverse = jnp.argsort(owners, axis=1)
    my_tiles = lax.dynamic_index_in_dim(inverse, my_index, 0, keepdims=False)
    outgoing = jnp.take(tile_block, my_tiles, axis=0)
    source_tiles = lax.dynamic_index_in_dim(inverse, my_index, 1, keepdims=False)
    held_rows = jnp.take_along_axis(counts, source_tiles[:, None], axis=1)[:, 0]
    inclusive = jnp.cumsum(held_rows)
    exclusive = inclusive - held_rows
    positions = jnp.arange(RECV, dtype=jnp.int32)
    source = jnp.sum((inclusive[None, :] <= positions[:, None]).astype(jnp.int32), axis=1)
    chosen = source[:, None] == jnp.arange(groups, dtype=jnp.int32)[None, :]
    slot_index = positions - jnp.sum(jnp.where(chosen, exclusive[None, :], 0), axis=1)
    flat_index = source * slots + slot_index
    outgoing, flat_index, here = together(outgoing, flat_index, here)
    incoming = lax.all_to_all(outgoing, ("zl", "x"), split_axis=0, concat_axis=0, tiled=True)
    packed = jnp.take(incoming.reshape(groups * slots, PART), flat_index, axis=0)

    gains = jnp.broadcast_to(ln_gain[None, :], (GAIN_ROWS, PART))
    mine = jnp.concatenate([packed, gains], axis=0)
    other = shift(mine, "zh", 2, 1)
    other, near = together(other, near)
    pieces = [here, own, *near, *far]
    rows = [lax.all_gather(part, ("y", "c"), axis=0) for part in (mine, other)]
    axes = [lax.axis_index(axis) for axis in ("x", "zh", "zl")]
    return mlp(jnp.stack(axes).astype(jnp.int32), rows, up_bias[None, :], pieces)


def solution(mesh):
    fine = Mesh(mesh.devices.reshape(8, 4, 2, 4, 2), ("zl", "x", "zh", "y", "c"))
    dp, mp = ("zl", "x"), ("zh", "y", "c")
    return jax.shard_map(
        local,
        mesh=fine,
        in_specs=(P(dp, mp), P(), P(), P(mp), P(dp, mp), P(mp)),
        out_specs=P(dp, mp),
        check_vma=False,
    )
```
